32 devices in a mesh: ctx: 8 (over z, x), pipe: 4 (over y, core).
Axes of the slice: x: 2, y: 2, z: 4, core: 2. Of those that a mesh axis runs over, the one named last changes fastest.
Arguments:
- section_out: bfloat16 [4, 1024, 4096], P('pipe', 'ctx'), may hold values from -6 to 6
- stash: bfloat16 [4, 1024, 4096], P('pipe', 'ctx'), may hold values from -6 to 6
- grad_out: bfloat16 [4, 1024, 4096], P('pipe', 'ctx'), may hold values from -6 to 6
- taps: float32 [4, 3, 7, 4096], P('pipe'), may hold values from -2 to 2
- residues: float32 [4, 16, 256], P('pipe'), may hold values from -2 to 2
- decays: float32 [4, 16, 256], P('pipe'), may hold values from 0.0002 to 0.1
- doc_lengths: int32 [2, 24], replicated, may hold values from 1 to 64, 1024 in all within a row
Outputs:
- mixed: bfloat16 [4, 1024, 4096], P('pipe', 'ctx')
- input_grad: bfloat16 [4, 1024, 4096], P('pipe', 'ctx')
- filter_grad: float32 [4, 16, 256], P('pipe')
- tap_grad: float32 [4, 3, 7, 4096], P('pipe')
The draws below stay inside these ranges and needn't reach their ends.
Inputs may be any that keep to these rules, and one draw needn't show every extreme that they name: `doc_lengths`: each row sums to 1024 and its largest length is exactly 64.
All inputs are finite; a program needn't handle non-finite values.
Results may differ from the reference program's by a relative error of at most 0.001.
Values may be sent and summed in bfloat16 or wider, within the bound.
A program may use at most 256 MiB of HBM per device.

```python
import math
import jax
import jax.numpy as jnp
import numpy as np
from jax import lax

CHANNELS = 4096
GROUP = 16
MODES = 16
TAPS = 7
NDOCS = 24
FILTERS = 256
SEQ = 1024
SECTIONS = 4
MAXDOC = 64


def draw_decays(key, part):
    key_pick, key_rate = jax.random.split(key)
    shape = (SECTIONS, MODES, FILTERS)
    pick = jax.random.uniform(key_pick, shape, jnp.float32)
    slow = pick < 0.5
    spread = jax.random.uniform(key_rate, shape, jnp.float32)
    slow_rate = jnp.exp(jnp.log(0.0002) + spread * (jnp.log(0.004) - jnp.log(0.0002)))
    fast_rate = 0.05 + spread * 0.05
    return jnp.where(slow, slow_rate, fast_rate).astype(jnp.float32)


def shard_levels(own_key, extent, cuts, smallest, largest):
    level, own = 1.0, jax.random.fold_in(own_key, 6)
    for dim, shards_of in cuts:
        steps = jnp.exp(jax.random.uniform(jax.random.fold_in(own, dim), (shards_of,), jnp.float32, smallest / len(cuts), largest / len(cuts)))
        level = level * jnp.repeat(steps, extent[dim] // shards_of).reshape([-1 if axis == dim else 1 for axis in range(len(extent))])
    return level


def length_profile(count, total, limit, skew):
    portions = [(1 << 20) // math.isqrt(rank ** skew) + 1 for rank in range(2, count + 1)]
    spare, counts = total - limit - (count - 1), [1] * (count - 1)
    while spare > 0:
        movable = [i for i in range(count - 1) if counts[i] < limit]
        whole, remaining = sum([portions[i] for i in movable]), spare
        for i in movable:
            extra = min(limit - counts[i], max(1, remaining * portions[i] // whole), spare)
            counts[i] = counts[i] + extra
            spare = spare - extra
    return np.array([limit] + counts)


def ragged_sizes(rng, amount, total, reach, skew):
    if amount == 2:
        one = jax.random.randint(rng, (), max(1, total - reach), min(reach, total - 1) + 1)
        return jnp.stack([one, total - one])
    sizes = jnp.asarray(length_profile(amount, total, reach, skew), jnp.int32)
    couples = (amount - 1) // 2
    donor, taker = sizes[1:1 + 2 * couples:2], sizes[2:2 + 2 * couples:2]
    margin = jnp.minimum(donor - 1, reach - taker)
    moved = jax.random.randint(jax.random.fold_in(rng, 1), (couples,), 0, 1 << 20) % (margin + 1)
    sizes = sizes.at[1:1 + 2 * couples:2].set(donor - moved).at[2:2 + 2 * couples:2].set(taker + moved)
    return sizes[jax.random.permutation(jax.random.fold_in(rng, 2), amount)]


def bell_draw(own_key, shape, scale, bound, cuts=(), kind=jnp.bfloat16):
    array = jax.random.normal(own_key, shape, jnp.float32) * scale
    if len(cuts) > 0:
        array = shard_levels(own_key, shape, cuts, -0.22, 0.18) * array
    return jnp.clip(array, min=-bound, max=bound).astype(kind)


def setup_inputs(seed: int = 0) -> dict:
    seeds = jax.random.split(jax.random.key(seed), 8)
    return {
        "section_out": bell_draw(seeds[0], (SECTIONS, SEQ, CHANNELS), 1.0, 6.0, ((0, 4), (1, 8))),
        "stash": bell_draw(seeds[1], (SECTIONS, SEQ, CHANNELS), 1.0, 6.0, ((0, 4), (1, 8))),
        "grad_out": bell_draw(seeds[2], (SECTIONS, SEQ, CHANNELS), 1.0, 6.0, ((0, 4), (1, 8))),
        "taps": bell_draw(seeds[3], (SECTIONS, 3, TAPS, CHANNELS), TAPS ** -0.5, 2.0, ((0, 4),), jnp.float32),
        "residues": bell_draw(seeds[4], (SECTIONS, MODES, FILTERS), 0.15, 2.0, ((0, 4),), jnp.float32),
        "decays": draw_decays(jax.random.fold_in(seeds[7], 71), 0),
        "doc_lengths": jax.vmap(lambda own: ragged_sizes(own, NDOCS, SEQ, MAXDOC, 2))(jax.random.split(seeds[6], 2)).reshape((2, NDOCS)).astype(jnp.int32),
    }


def doc_ids(lengths):
    starts = jnp.cumsum(lengths) - lengths
    places = jnp.arange(SEQ, dtype=jnp.int32)
    return lax.optimization_barrier(jnp.sum((starts[None, :] <= places[:, None]).astype(jnp.int32), axis=1)) - 1

def shift_down(values, j):
    if j == 0:
        return values
    return jnp.concatenate([jnp.zeros((j,) + values.shape[1:], values.dtype), values[:-j]], axis=0)

def shift_up(values, j):
    if j == 0:
        return values
    return jnp.concatenate([values[j:], jnp.zeros((j,) + values.shape[1:], values.dtype)], axis=0)

def doc_down(docs, j):
    if j == 0:
        return docs
    return jnp.concatenate([jnp.full((j,), -1, jnp.int32), docs[:-j]]).astype(jnp.int32)

def doc_up(docs, j):
    if j == 0:
        return docs
    return jnp.concatenate([docs[j:], jnp.full((j,), -2, jnp.int32)]).astype(jnp.int32)

def featurize(values, taps_here, docs):
    result = jnp.zeros((3,) + values.shape, jnp.float32)
    for j in range(TAPS):
        valid = (doc_down(docs, j) == docs).astype(jnp.float32)
        result = result + taps_here[:, j][:, None, :] * (shift_down(values, j) * valid[:, None])[None]
    return result

def modal_forward(source, rate_c, resid_c, reset):
    decay = jnp.exp(-rate_c)

    def step(state, inputs):
        value, flag = inputs
        state = state * decay * (1.0 - flag) + value[None, :]
        return (state, lax.optimization_barrier(jnp.sum(resid_c * state, axis=0)))
    init = jnp.zeros(rate_c.shape, jnp.float32)
    _, out = lax.scan(step, init, (source, reset))
    return out

def modal_backward(source, rate_c, resid_c, reset):
    decay = jnp.exp(-rate_c)
    reset_next = jnp.concatenate([reset[1:], jnp.ones((1,), jnp.float32)])

    def step(state, inputs):
        value, flag = inputs
        state = state * decay * (1.0 - flag) + value[None, :]
        return (state, lax.optimization_barrier(jnp.sum(resid_c * state, axis=0)))
    init = jnp.zeros(rate_c.shape, jnp.float32)
    _, out = lax.scan(step, init, (source, reset_next), reverse=True)
    return out

def modal_grad(source, cotan, rate_c, reset):
    decay = jnp.exp(-rate_c)

    def step(carry, inputs):
        state, total = carry
        value, grad_value, flag = inputs
        state = state * decay * (1.0 - flag) + value[None, :]
        total = total + grad_value[None, :] * state
        return ((state, total), None)
    init = (jnp.zeros(rate_c.shape, jnp.float32), jnp.zeros(rate_c.shape, jnp.float32))
    (state, total), _ = lax.scan(step, init, (source, cotan, reset))
    return total

def reference(section_out, stash, grad_out, taps, residues, decays, doc_lengths):
    docs_new = doc_ids(doc_lengths[0])
    docs_old = doc_ids(doc_lengths[1])
    reset_new = (docs_new != doc_down(docs_new, 1)).astype(jnp.float32)
    reset_old = (docs_old != doc_down(docs_old, 1)).astype(jnp.float32)
    mixed_all, input_all, filter_all, tap_all = ([], [], [], [])
    for p in range(SECTIONS):
        x_new = section_out[(p - 1) % SECTIONS].astype(jnp.float32)
        x_old = stash[p].astype(jnp.float32)
        upstream = grad_out[(p + 1) % SECTIONS].astype(jnp.float32)
        rate_c = jnp.repeat(decays[p], GROUP, axis=1)
        resid_c = jnp.repeat(residues[p], GROUP, axis=1)
        feat_new = featurize(x_new, taps[p], docs_new)
        long_new = modal_forward(feat_new[1] * feat_new[2], rate_c, resid_c, reset_new)
        mixed_all.append((feat_new[0] * long_new).astype(jnp.bfloat16))
        feat_old = featurize(x_old, taps[p], docs_old)
        gated_old = feat_old[1] * feat_old[2]
        long_old = modal_forward(gated_old, rate_c, resid_c, reset_old)
        grad_q = upstream * long_old
        grad_long = upstream * feat_old[0]
        grad_gated = modal_backward(grad_long, rate_c, resid_c, reset_old)
        grads = jnp.stack([grad_q, grad_gated * feat_old[2], grad_gated * feat_old[1]])
        total = modal_grad(gated_old, grad_long, rate_c, reset_old)
        filter_all.append(lax.optimization_barrier(jnp.sum(total.reshape(MODES, FILTERS, GROUP), axis=2)))
        back = jnp.zeros(x_old.shape, jnp.float32)
        tap_rows = []
        for j in range(TAPS):
            valid_up = (doc_up(docs_old, j) == docs_old).astype(jnp.float32)
            for i in range(3):
                back = back + taps[p, i, j][None, :] * shift_up(grads[i], j) * valid_up[:, None]
            valid_down = (doc_down(docs_old, j) == docs_old).astype(jnp.float32)
            moved = shift_down(x_old, j) * valid_down[:, None]
            tap_rows.append(lax.optimization_barrier(jnp.sum(grads * moved[None], axis=1)))
        input_all.append(back.astype(jnp.bfloat16))
        tap_all.append(jnp.stack(tap_rows, axis=1))
    return (jnp.stack(mixed_all), jnp.stack(input_all), jnp.stack(filter_all), jnp.stack(tap_all))
```

```python
import functools
import jax
import jax.numpy as jnp
from jax import lax
from jax.experimental import pallas as pl
from jax.experimental.pallas import tpu as pltpu
from jax.sharding import PartitionSpec as P

F32 = jnp.float32
UNROLL = 4
LANES = 128
SUB = 8
BLOCK = LANES * SUB


def from_behind(value, axis, steps):
    count = lax.axis_size(axis)
    initial, last = (max(0, -steps), min(count, count - steps))
    return lax.ppermute(value, axis, [(source, source + steps) for source in range(initial, last)])


def passed_along(array, axis, by):
    count = lax.axis_size(axis)
    return lax.ppermute(array, axis, [(i, (i + by) % count) for i in range(count)])


def doc_meta(lengths, base, rows):
    starts = jnp.cumsum(lengths) - lengths
    places = base + jnp.arange(rows + 16, dtype=jnp.int32)
    far = jnp.int32(1 << 30)
    gaps = places[:, None] - starts[None, :]
    age = jnp.min(jnp.where(gaps >= 0, gaps, far), axis=1)
    keep = (age > 0).astype(jnp.int32)
    positions = jnp.arange(rows, dtype=jnp.int32)
    fresh = age[:rows] == 0
    first = jnp.min(jnp.where(fresh, positions, rows))
    last = jnp.max(jnp.where(fresh, positions, -1))
    through = first == rows
    u = UNROLL
    front_hi = (first + u - 1) // u
    main_lo = jnp.where(through, 0, first // u)
    main_hi = jnp.where(through, rows // u, (last + u - 1) // u)
    tail_lo = jnp.maximum(last, 0) // u
    bounds = jnp.stack([front_hi, main_lo, main_hi, tail_lo, last, age[0]]).astype(jnp.int32)
    return jnp.concatenate([bounds, jnp.zeros((2,), jnp.int32), keep]), through.astype(F32)


HEAD = 8


def at(ref, t):
    return ref[pl.ds(pl.multiple_of(t * SUB, SUB), SUB), :]


def put(ref, t, value):
    ref[pl.ds(pl.multiple_of(t * SUB, SUB), SUB), :] = value


def scatter_rows(src, dst, rows, offset):
    def body(g, _):
        for c in range(SUB):
            tile = src[pl.ds(pl.multiple_of(g * 16, 16), 16), c * LANES : (c + 1) * LANES].astype(F32)
            for h in range(2):
                dst[pl.ds((offset + g * 16 + h * 8) * SUB + c, 8, stride=SUB), :] = tile[h * 8 : h * 8 + 8]
        return 0

    lax.fori_loop(0, rows // 16, body, 0)


def gather_rows(src, dst, rows):
    def body(g, _):
        for c in range(SUB):
            halves = [src[pl.ds((g * 16 + h * 8) * SUB + c, 8, stride=SUB), :] for h in range(2)]
            dst[pl.ds(pl.multiple_of(g * 16, 16), 16), c * LANES : (c + 1) * LANES] = jnp.concatenate(
                halves, axis=0
            ).astype(dst.dtype)
        return 0

    lax.fori_loop(0, rows // 16, body, 0)


def total_of(parts):
    while len(parts) > 1:
        parts = [a + b for a, b in zip(parts[::2], parts[1::2])] + ([parts[-1]] if len(parts) % 2 else [])
    return parts[0]


def decayed(dtab, flag, states, value):
    modes = len(states)
    return [
        states[m] * dtab[pl.ds(pl.multiple_of(flag * (modes * SUB) + m * SUB, SUB), SUB), :] + value
        for m in range(modes)
    ]


def load_states(ref, modes):
    return tuple(at(ref, m) for m in range(modes))


def scan_forward(meta, source, dtab, resid, lo, hi, init, emit):
    modes = len(init)

    def body(g, states):
        states = list(states)
        for u in range(UNROLL):
            t = g * UNROLL + u
            states = decayed(dtab, meta[HEAD + t], states, at(source, t))
            emit(t, total_of([at(resid, m) * states[m] for m in range(modes)]))
        return tuple(states)

    return lax.fori_loop(lo, hi, body, init)


def scan_backward(meta, cotan, source, dtab, resid, lo, hi, init, totals, weight, emit):
    modes = len(init)

    def body(i, carry):
        states, sums = list(carry[0]), list(carry[1])
        g = hi - 1 - i
        for u in reversed(range(UNROLL)):
            t = g * UNROLL + u
            states = decayed(dtab, meta[HEAD + t + 1], states, at(cotan, t))
            emit(t, total_of([at(resid, m) * states[m] for m in range(modes)]))
            value = at(source, t) * weight(t)
            sums = [sums[m] + value * states[m] for m in range(modes)]
        return tuple(states), tuple(sums)

    return lax.fori_loop(0, hi - lo, body, (init, totals))


def forward_kernel(rows, modes, taps_count, meta, x, rim, taps, dtab, resid, *outs, full):
    if full:
        xs, qs, ks, vs, gs, longs, end = outs
    else:
        qs, gs, longs, end, xs = outs
    for c in range(SUB):
        xs[pl.ds(c, 8, stride=SUB), :] = rim[:, c * LANES : (c + 1) * LANES].astype(F32)
    scatter_rows(x, xs, rows, 8)
    age = meta[5]
    window = tuple(
        at(xs, 8 - j) * jnp.where(age >= j, 1.0, 0.0).astype(F32) for j in range(1, taps_count)
    )

    def feats(g, window):
        window = list(window)
        for u in range(2):
            t = g * 2 + u
            keep = meta[HEAD + t].astype(F32)
            now = at(xs, t + 8)
            seen = [now] + [w * keep for w in window]
            q, k, v = [
                total_of([at(taps, i * taps_count + j) * seen[j] for j in range(taps_count)])
                for i in range(3)
            ]
            put(qs, t, q)
            put(gs, t, k * v)
            if full:
                put(ks, t, k)
                put(vs, t, v)
            window = seen[:-1]
        return tuple(window)

    lax.fori_loop(0, rows // 2, feats, window)
    init = tuple(jnp.zeros((SUB, LANES), F32) for _ in range(modes))
    states = scan_forward(
        meta, gs, dtab, resid, meta[1], rows // UNROLL, init, lambda t, y: put(longs, t, y)
    )
    for m in range(modes):
        put(end, m, states[m])


def mixed_kernel(rows, modes, meta, qs, gs, longs, state, dtab, resid, out, scratch):
    def product(g, _):
        for u in range(8):
            t = g * 8 + u
            put(scratch, t, at(qs, t) * at(longs, t))
        return 0

    lax.fori_loop(0, rows // 8, product, 0)
    scan_forward(
        meta, gs, dtab, resid, 0, meta[0], load_states(state, modes),
        lambda t, y: put(scratch, t, y * at(qs, t)),
    )
    gather_rows(scratch, out, rows)


def backward_kernel(
    rows, modes, meta, up, qs, ks, vs, gs, longs, state, dtab, resid,
    dq, dl, dg, begin, sums, rim, ups,
):
    scatter_rows(up, ups, rows, 0)

    def product(g, _):
        for u in range(8):
            t = g * 8 + u
            value = at(ups, t)
            put(dq, t, value * at(longs, t))
            put(dl, t, value * at(qs, t))
            put(dg, t, jnp.zeros((SUB, LANES), F32))
        return 0

    lax.fori_loop(0, rows // 8, product, 0)
    scan_forward(
        meta, gs, dtab, resid, 0, meta[0], load_states(state, modes),
        lambda t, y: put(dq, t, y * at(ups, t)),
    )
    zeros = tuple(jnp.zeros((SUB, LANES), F32) for _ in range(modes))
    last = meta[4]
    states, totals = scan_backward(
        meta, dl, gs, dtab, resid, 0, meta[2], zeros, zeros,
        lambda t: jnp.where(t < last, 1.0, 0.0).astype(F32),
        lambda t, y: put(dg, t, y),
    )
    for m in range(modes):
        put(begin, m, states[m])
        put(sums, m, totals[m])
    for t in range(8):
        value = at(dg, t)
        put(rim, t, at(dq, t))
        put(rim, 8 + t, value * at(vs, t))
        put(rim, 16 + t, value * at(ks, t))


def finish_kernel(
    rows, modes, taps_count, meta, xs, ks, vs, gs, dq, dl, dg, rim, state, sums, taps, dtab, resid,
    out, tap_out, sums_out, dks, dvs, backs,
):
    def copy(g, _):
        for u in range(8):
            put(dks, g * 8 + u, at(dg, g * 8 + u))
        return 0

    lax.fori_loop(0, rows // 8, copy, 0)
    last = meta[4]
    _, totals = scan_backward(
        meta, dl, gs, dtab, resid, meta[3], rows // UNROLL, load_states(state, modes),
        load_states(sums, modes),
        lambda t: jnp.where(t >= last, 1.0, 0.0).astype(F32),
        lambda t, y: put(dks, t, y),
    )
    for m in range(modes):
        put(sums_out, m, totals[m])

    def spread(pending, grads, keep):
        parts = [
            total_of([at(taps, i * taps_count + j) * grads[i] for i in range(3)])
            for j in range(taps_count)
        ]
        done = pending[0] + parts[0]
        later = list(pending[1:]) + [None]
        return done, tuple(
            ((parts[k + 1] + later[k]) if later[k] is not None else parts[k + 1]) * keep
            for k in range(taps_count - 1)
        )

    pending = tuple(jnp.zeros((SUB, LANES), F32) for _ in range(taps_count - 1))
    for r in reversed(range(taps_count - 1)):
        grads = [at(rim, i * 8 + r) for i in range(3)]
        _, pending = spread(pending, grads, meta[HEAD + rows + r].astype(F32))

    def descend(i, pending):
        g = rows // 2 - 1 - i
        for u in reversed(range(2)):
            t = g * 2 + u
            gated = at(dks, t)
            dk = gated * at(vs, t)
            dv = gated * at(ks, t)
            put(dks, t, dk)
            put(dvs, t, dv)
            done, pending = spread(pending, [at(dq, t), dk, dv], meta[HEAD + t].astype(F32))
            put(backs, t, done)
        return pending

    lax.fori_loop(0, rows // 2, descend, pending)
    gather_rows(backs, out, rows)
    age = meta[5]
    window = tuple(
        at(xs, 8 - j) * jnp.where(age >= j, 1.0, 0.0).astype(F32) for j in range(1, taps_count)
    )
    zeros = tuple(jnp.zeros((SUB, LANES), F32) for _ in range(3 * taps_count))

    def ascend(g, carry):
        window, acc = list(carry[0]), list(carry[1])
        for u in range(2):
            t = g * 2 + u
            keep = meta[HEAD + t].astype(F32)
            seen = [at(xs, t + 8)] + [w * keep for w in window]
            grads = [at(dq, t), at(dks, t), at(dvs, t)]
            acc = [
                acc[i * taps_count + j] + grads[i] * seen[j]
                for i in range(3)
                for j in range(taps_count)
            ]
            window = seen[:-1]
        return tuple(window), tuple(acc)

    _, acc = lax.fori_loop(0, rows // 2, ascend, (window, zeros))
    for n in range(3 * taps_count):
        put(tap_out, n, acc[n])


def on_device(section_out, stash, grad_out, taps, residues, decays, doc_lengths):
    stashed = stash[0]
    rows, width = stashed.shape
    modes, filters = residues.shape[1:]
    branches, taps_count = taps.shape[1:3]
    group = width // filters
    blocks = width // BLOCK
    ctx_size = lax.axis_size("ctx")
    pipe_size = lax.axis_size("pipe")
    base = lax.axis_index("ctx") * rows
    span = rows * ctx_size // 16 // rows + 1
    depth = (span - 1).bit_length()

    upstream = passed_along(grad_out, "pipe", -1)[0]
    incoming = passed_along(section_out, "pipe", 1)[0]
    rim_old = from_behind(stashed[rows - 8 :], "ctx", 1)
    rim_new = from_behind(passed_along(section_out[0, rows - 8 :], "pipe", 1), "ctx", 1)

    meta_new, through_new = doc_meta(doc_lengths[0], base, rows)
    meta_old, through_old = doc_meta(doc_lengths[1], base, rows)

    def expand(small):
        wide = jnp.broadcast_to(small[:, :, None], (modes, filters, group)).reshape(modes, blocks, SUB, LANES)
        return jnp.swapaxes(wide, 0, 1).reshape(blocks, modes * SUB, LANES)

    rates = expand(decays[0])
    resid = expand(residues[0])
    decay = jnp.exp(-rates)
    dtab = jnp.concatenate([jnp.zeros_like(decay), decay], axis=1)
    tapped = jnp.swapaxes(taps[0].reshape(branches * taps_count, blocks, SUB, LANES), 0, 1)
    tapped = tapped.reshape(blocks, branches * taps_count * SUB, LANES)

    smem = pl.BlockSpec(memory_space=pltpu.SMEM)
    tokens = pl.BlockSpec((rows, BLOCK), lambda b: (0, b))
    edge = pl.BlockSpec((8, BLOCK), lambda b: (0, b))

    def major(count):
        return pl.BlockSpec((None, count * SUB, LANES), lambda b: (b, 0, 0))

    def shaped(count):
        return jax.ShapeDtypeStruct((blocks, count * SUB, LANES), F32)

    def scratch(count):
        return pltpu.VMEM((count * SUB, LANES), F32)

    def cost(ops, count):
        return pl.CostEstimate(flops=ops * rows * width, bytes_accessed=4 * count * rows * width, transcendentals=0)

    wide = jax.ShapeDtypeStruct((rows, width), jnp.bfloat16)
    tail = [major(branches * taps_count), major(2 * modes), major(modes)]

    def link(earlier, later):
        return (earlier[0] * later[0], later[0] * earlier[1] + later[1])

    def nearby(through, summary, sign):
        if depth == 0:
            return from_behind(summary, "ctx", sign)
        current = (through * jnp.exp(-rates * rows), summary)
        for j in range(depth + 1):
            reach = 1 if j == 0 else 2 ** (j - 1)
            moved = from_behind(current, "ctx", sign * reach)
            current = moved if j == 0 else link(moved, current)
        return current[1]

    xs, qs, ks, vs, gs, longs, end_old = pl.pallas_call(
        functools.partial(forward_kernel, rows, modes, taps_count, full=True),
        grid=(blocks,),
        in_specs=[smem, tokens, edge] + tail,
        out_specs=[major(rows + 8)] + [major(rows)] * 5 + [major(modes)],
        out_shape=[shaped(rows + 8)] + [shaped(rows)] * 5 + [shaped(modes)],
        cost_estimate=cost(110, 7),
        name="forward_old",
    )(meta_old, stashed, rim_old, tapped, dtab, resid)
    state_old = nearby(through_old, end_old, 1)

    qn, gn, longn, end_new = pl.pallas_call(
        functools.partial(forward_kernel, rows, modes, taps_count, full=False),
        grid=(blocks,),
        in_specs=[smem, tokens, edge] + tail,
        out_specs=[major(rows)] * 3 + [major(modes)],
        out_shape=[shaped(rows)] * 3 + [shaped(modes)],
        scratch_shapes=[scratch(rows + 8)],
        cost_estimate=cost(110, 4),
        name="forward_new",
    )(meta_new, incoming, rim_new, tapped, dtab, resid)
    state_new = nearby(through_new, end_new, 1)

    dq, dl, dg, begin, sums, rim = pl.pallas_call(
        functools.partial(backward_kernel, rows, modes),
        grid=(blocks,),
        in_specs=[smem, tokens] + [major(rows)] * 5 + [major(modes)] + tail[1:],
        out_specs=[major(rows)] * 3 + [major(modes)] * 2 + [major(24)],
        out_shape=[shaped(rows)] * 3 + [shaped(modes)] * 2 + [shaped(24)],
        scratch_shapes=[scratch(rows)],
        cost_estimate=cost(120, 8),
        name="backward_main",
    )(meta_old, upstream, qs, ks, vs, gs, longs, state_old, dtab, resid)
    later = nearby(through_old, begin, -1)
    if depth > 0:
        reach = (rows - jnp.arange(8, dtype=F32))[None, :, None, None, None]
        spread = (blocks, modes, SUB, LANES)
        extra = jnp.sum(
            (resid * later).reshape(spread)[:, None]
            * jnp.exp(-rates.reshape(spread)[:, None] * jnp.swapaxes(reach, 2, 2)),
            axis=2,
        ).reshape(blocks, 8 * SUB, LANES) * through_old
        head = 8 * SUB
        rim = rim + jnp.concatenate(
            [jnp.zeros_like(extra), extra * vs[:, :head], extra * ks[:, :head]], axis=1
        )
    rim_in = from_behind(rim, "ctx", -1)

    mixed = pl.pallas_call(
        functools.partial(mixed_kernel, rows, modes),
        grid=(blocks,),
        in_specs=[smem] + [major(rows)] * 3 + [major(modes)] + tail[1:],
        out_specs=tokens,
        out_shape=wide,
        scratch_shapes=[scratch(rows)],
        cost_estimate=cost(30, 4),
        name="mixed",
    )(meta_new, qn, gn, longn, state_new, dtab, resid)

    back, tap_term, totals = pl.pallas_call(
        functools.partial(finish_kernel, rows, modes, taps_count),
        grid=(blocks,),
        in_specs=[smem, major(rows + 8)] + [major(rows)] * 6 + [major(24)] + [major(modes)] * 2 + tail,
        out_specs=[tokens, major(branches * taps_count), major(modes)],
        out_shape=[wide, shaped(branches * taps_count), shaped(modes)],
        scratch_shapes=[scratch(rows)] * 3,
        cost_estimate=cost(150, 8),
        name="finish",
    )(meta_old, xs, ks, vs, gs, dq, dl, dg, rim_in, later, sums, tapped, dtab, resid)

    filter_term = jnp.sum(
        jnp.swapaxes(totals.reshape(blocks, modes, SUB, LANES), 0, 1).reshape(modes, filters, group), axis=2
    )
    tap_term = jnp.swapaxes(tap_term.reshape(blocks, branches * taps_count, SUB, LANES), 0, 1).reshape(
        branches, taps_count, width
    )
    summed = lax.psum((filter_term, tap_term), "ctx")
    return (mixed[None], back[None], summed[0][None], summed[1][None])


def solution(mesh):
    in_specs = (
        P("pipe", "ctx", None),
        P("pipe", "ctx", None),
        P("pipe", "ctx", None),
        P("pipe", None, None, None),
        P("pipe", None, None),
        P("pipe", None, None),
        P(),
    )
    out_specs = (
        P("pipe", "ctx", None),
        P("pipe", "ctx", None),
        P("pipe", None, None),
        P("pipe", None, None, None),
    )
    return jax.shard_map(
        on_device, mesh=mesh, in_specs=in_specs, out_specs=out_specs, check_vma=False
    )
```

```python
import functools
import jax
import jax.numpy as jnp
from jax import lax
from jax.experimental import pallas as pl
from jax.experimental.pallas import tpu as pltpu
from jax.sharding import PartitionSpec as P

F32 = jnp.float32
SHIFT = 2
UNROLL = 1 << SHIFT
LANES = 128
SUB = 8
BLOCK = LANES * SUB


def from_behind(value, axis, steps):
    count = lax.axis_size(axis)
    initial, last = (max(0, -steps), min(count, count - steps))
    return lax.ppermute(value, axis, [(source, source + steps) for source in range(initial, last)])


def passed_along(array, axis, by):
    count = lax.axis_size(axis)
    return lax.ppermute(array, axis, [(i, (i + by) % count) for i in range(count)])


HEAD = 8


def at(ref, t):
    return ref[pl.ds(pl.multiple_of(t * SUB, SUB), SUB), :]


def put(ref, t, value):
    ref[pl.ds(pl.multiple_of(t * SUB, SUB), SUB), :] = value


def scatter_rows(src, dst, rows, offset):
    def body(g, _):
        for c in range(SUB):
            tile = src[pl.ds(pl.multiple_of(g * 16, 16), 16), c * LANES : (c + 1) * LANES].astype(F32)
            for h in range(2):
                dst[pl.ds((offset + g * 16 + h * 8) * SUB + c, 8, stride=SUB), :] = tile[h * 8 : h * 8 + 8]
        return 0

    lax.fori_loop(0, rows // 16, body, 0)


def gather_rows(src, dst, rows):
    def body(g, _):
        for c in range(SUB):
            halves = [src[pl.ds((g * 16 + h * 8) * SUB + c, 8, stride=SUB), :] for h in range(2)]
            dst[pl.ds(pl.multiple_of(g * 16, 16), 16), c * LANES : (c + 1) * LANES] = jnp.concatenate(
                halves, axis=0
            ).astype(dst.dtype)
        return 0

    lax.fori_loop(0, rows // 16, body, 0)


def total_of(parts):
    while len(parts) > 1:
        parts = [a + b for a, b in zip(parts[::2], parts[1::2])] + ([parts[-1]] if len(parts) % 2 else [])
    return parts[0]


def decayed(dtab, flag, states, value):
    modes = len(states)
    return [
        states[m] * dtab[pl.ds(pl.multiple_of(flag * (modes * SUB) + m * SUB, SUB), SUB), :] + value
        for m in range(modes)
    ]


def load_states(ref, modes):
    return tuple(at(ref, m) for m in range(modes))


def scan_forward(meta, source, dtab, resid, lo, hi, init, emit):
    modes = len(init)

    def body(g, states):
        states = list(states)
        for u in range(UNROLL):
            t = g * UNROLL + u
            states = decayed(dtab, meta[HEAD + t], states, at(source, t))
            emit(t, total_of([at(resid, m) * states[m] for m in range(modes)]))
        return tuple(states)

    return lax.fori_loop(lo, hi, body, init)


def scan_backward(meta, cotan, source, dtab, resid, lo, hi, init, totals, weight, emit):
    modes = len(init)

    def body(i, carry):
        states, sums = list(carry[0]), list(carry[1])
        g = hi - 1 - i
        for u in reversed(range(UNROLL)):
            t = g * UNROLL + u
            states = decayed(dtab, meta[HEAD + t + 1], states, at(cotan, t))
            emit(t, total_of([at(resid, m) * states[m] for m in range(modes)]))
            value = at(source, t) * weight(t)
            sums = [sums[m] + value * states[m] for m in range(modes)]
        return tuple(states), tuple(sums)

    return lax.fori_loop(0, hi - lo, body, (init, totals))


def forward_kernel(rows, modes, taps_count, meta, x, rim, taps, dtab, resid, *outs, full):
    if full:
        xs, qs, ks, vs, gs, longs, end = outs
    else:
        qs, gs, longs, end, xs = outs
    for c in range(SUB):
        xs[pl.ds(c, 8, stride=SUB), :] = rim[:, c * LANES : (c + 1) * LANES].astype(F32)
    scatter_rows(x, xs, rows, 8)
    age = meta[5]
    window = tuple(
        at(xs, 8 - j) * jnp.where(age >= j, 1.0, 0.0).astype(F32) for j in range(1, taps_count)
    )

    def feats(g, window):
        window = list(window)
        for u in range(2):
            t = g * 2 + u
            keep = meta[HEAD + t].astype(F32)
            now = at(xs, t + 8)
            seen = [now] + [w * keep for w in window]
            q, k, v = [
                total_of([taps[i * taps_count + j] * seen[j] for j in range(taps_count)])
                for i in range(3)
            ]
            put(qs, t, q)
            put(gs, t, k * v)
            if full:
                put(ks, t, k)
                put(vs, t, v)
            window = seen[:-1]
        return tuple(window)

    lax.fori_loop(0, rows // 2, feats, window)
    init = tuple(jnp.zeros((SUB, LANES), F32) for _ in range(modes))
    states = scan_forward(
        meta, gs, dtab, resid, meta[1], rows // UNROLL, init, lambda t, y: put(longs, t, y)
    )
    for m in range(modes):
        put(end, m, states[m])


def mixed_kernel(rows, modes, meta, qs, gs, longs, state, dtab, resid, out, scratch):
    def product(g, _):
        for u in range(8):
            t = g * 8 + u
            put(scratch, t, at(qs, t) * at(longs, t))
        return 0

    lax.fori_loop(0, rows // 8, product, 0)
    scan_forward(
        meta, gs, dtab, resid, 0, meta[0], load_states(state, modes),
        lambda t, y: put(scratch, t, y * at(qs, t)),
    )
    gather_rows(scratch, out, rows)


def backward_kernel(
    rows, modes, meta, up, qs, ks, vs, gs, longs, state, dtab, resid, after,
    dq, dl, dg, begin, sums, rim, ups,
):
    scatter_rows(up, ups, rows, 0)

    def product(g, _):
        for u in range(8):
            t = g * 8 + u
            value = at(ups, t)
            put(dq, t, value * at(longs, t))
            put(dl, t, value * at(qs, t))
            put(dg, t, jnp.zeros((SUB, LANES), F32))
        return 0

    lax.fori_loop(0, rows // 8, product, 0)
    scan_forward(
        meta, gs, dtab, resid, 0, meta[0], load_states(state, modes),
        lambda t, y: put(dq, t, y * at(ups, t)),
    )
    zeros = tuple(jnp.zeros((SUB, LANES), F32) for _ in range(modes))
    last = meta[4]
    states, totals = scan_backward(
        meta, dl, gs, dtab, resid, 0, meta[2], zeros, zeros,
        lambda t: jnp.where(t < last, 1.0, 0.0).astype(F32),
        lambda t, y: put(dg, t, y),
    )
    for m in range(modes):
        put(begin, m, states[m])
        put(sums, m, totals[m])
    for t in range(8):
        value = at(dg, t)
        put(rim, t, at(dq, t))
        put(rim, 8 + t, value * at(vs, t))
        put(rim, 16 + t, value * at(ks, t))


def finish_kernel(
    rows, modes, taps_count, group, meta, xs, ks, vs, gs, dq, dl, dg, rim, state, sums, taps, dtab, resid, after,
    out, tap_out, dks, dvs, backs,
):
    def copy(g, _):
        for u in range(8):
            put(dks, g * 8 + u, at(dg, g * 8 + u))
        return 0

    lax.fori_loop(0, rows // 8, copy, 0)
    last = meta[4]
    _, totals = scan_backward(
        meta, dl, gs, dtab, resid, meta[3], rows // UNROLL, load_states(state, modes),
        load_states(sums, modes),
        lambda t: jnp.where(t >= last, 1.0, 0.0).astype(F32),
        lambda t, y: put(dks, t, y),
    )
    lane = lax.broadcasted_iota(jnp.int32, (SUB, LANES), 1)
    groups = LANES // group
    filter_tile = jnp.zeros((SUB, LANES), F32)
    for m in range(modes):
        part, step = totals[m], 1
        while step < group:
            part = part + pltpu.roll(part, LANES - step, 1)
            step *= 2
        moved = jnp.take_along_axis(part, lane % groups * group, axis=1)
        filter_tile = jnp.where(lane // groups == m, moved, filter_tile)
    tap_out[3 * taps_count] = filter_tile

    def spread(pending, grads, keep):
        parts = [
            total_of([taps[i * taps_count + j] * grads[i] for i in range(3)])
            for j in range(taps_count)
        ]
        done = pending[0] + parts[0]
        later = list(pending[1:]) + [None]
        return done, tuple(
            ((parts[k + 1] + later[k]) if later[k] is not None else parts[k + 1]) * keep
            for k in range(taps_count - 1)
        )

    pending = tuple(jnp.zeros((SUB, LANES), F32) for _ in range(taps_count - 1))
    for r in reversed(range(taps_count - 1)):
        grads = [at(rim, i * 8 + r) for i in range(3)]
        _, pending = spread(pending, grads, meta[HEAD + rows + r].astype(F32))

    def descend(i, pending):
        g = rows // 2 - 1 - i
        for u in reversed(range(2)):
            t = g * 2 + u
            gated = at(dks, t)
            dk = gated * at(vs, t)
            dv = gated * at(ks, t)
            put(dks, t, dk)
            put(dvs, t, dv)
            done, pending = spread(pending, [at(dq, t), dk, dv], meta[HEAD + t].astype(F32))
            put(backs, t, done)
        return pending

    lax.fori_loop(0, rows // 2, descend, pending)
    gather_rows(backs, out, rows)
    age = meta[5]
    window = tuple(
        at(xs, 8 - j) * jnp.where(age >= j, 1.0, 0.0).astype(F32) for j in range(1, taps_count)
    )
    zeros = tuple(jnp.zeros((SUB, LANES), F32) for _ in range(3 * taps_count))

    def ascend(g, carry):
        window, acc = list(carry[0]), list(carry[1])
        for u in range(2):
            t = g * 2 + u
            keep = meta[HEAD + t].astype(F32)
            seen = [at(xs, t + 8)] + [w * keep for w in window]
            grads = [at(dq, t), at(dks, t), at(dvs, t)]
            acc = [
                acc[i * taps_count + j] + grads[i] * seen[j]
                for i in range(3)
                for j in range(taps_count)
            ]
            window = seen[:-1]
        return tuple(window), tuple(acc)

    _, acc = lax.fori_loop(0, rows // 2, ascend, (window, zeros))
    for n in range(3 * taps_count):
        tap_out[n] = acc[n]


def prepare_kernel(rows, blocks, lengths, rates, resids, meta_new, meta_old, dtab, resid):
    base = lax.axis_index("ctx") * rows
    reach = rows + 16
    for which, meta in enumerate((meta_new, meta_old)):

        def fill(i, _):
            for u in range(8):
                meta[i * 8 + u] = 1
            return 0

        lax.fori_loop(0, (HEAD + reach) // 8, fill, 0)

        def document(i, carry):
            offset, first, last, begin = carry
            inside = jnp.logical_and(offset >= 0, offset < reach)
            meta[jnp.where(inside, HEAD + offset, 7)] = 0
            first = jnp.where(offset >= 0, jnp.minimum(first, offset), first)
            last = jnp.where(jnp.logical_and(offset >= 0, offset < rows), offset, last)
            begin = jnp.where(offset <= 0, offset, begin)
            return offset + lengths[which, i], first, last, begin

        start = (-base, jnp.int32(rows), jnp.int32(-1), jnp.int32(0))
        _, first, last, begin = lax.fori_loop(0, lengths.shape[1], document, start)
        through = first == rows
        meta[0] = lax.shift_right_logical(first + (UNROLL - 1), SHIFT)
        meta[1] = jnp.where(through, 0, lax.shift_right_logical(first, SHIFT))
        meta[2] = jnp.where(through, rows // UNROLL, lax.shift_right_logical(last + (UNROLL - 1), SHIFT))
        meta[3] = lax.shift_right_logical(jnp.maximum(last, 0), SHIFT)
        meta[4] = last
        meta[5] = -begin
        meta[6] = jnp.where(through, 1, 0)
    modes, filters = rates.shape
    group = blocks * BLOCK // filters
    lane = lax.broadcasted_iota(jnp.int32, (modes, LANES), 1) // group
    zeros = jnp.zeros((modes * SUB, LANES), F32)
    for b in range(blocks):
        dtab[b, 0 : modes * SUB, :] = zeros
        for c in range(SUB):
            low = (b * SUB + c) * (LANES // group)
            tile, place = low // LANES * LANES, low % LANES
            for source, target, offset in ((rates, dtab, modes * SUB), (resids, resid, 0)):
                wide = jnp.take_along_axis(source[:, tile : tile + LANES], lane + place, axis=1)
                if target is dtab:
                    wide = jnp.exp(-wide)
                for h in range(0, modes, 8):
                    target[b, pl.ds(offset + h * SUB + c, 8, stride=SUB), :] = wide[h : h + 8]


def sum_kernel(count, chunk, own, out, inbox, send, arrive, share, gather):
    me = lax.axis_index("ctx")
    mine = pl.ds(me * chunk, chunk)
    mesh_ids = pl.DeviceIdType.MESH

    def peer_of(d):
        return lax.rem(me + d + 1, count)

    barrier = pltpu.get_barrier_semaphore()

    def greet(d, _):
        pl.semaphore_signal(barrier, inc=1, device_id={"ctx": peer_of(d)}, device_id_type=mesh_ids)
        return 0

    lax.fori_loop(0, count - 1, greet, 0)
    pl.semaphore_wait(barrier, count - 1)

    def piece(d):
        peer = peer_of(d)
        return pltpu.make_async_remote_copy(
            src_ref=own.at[pl.ds(peer * chunk, chunk)], dst_ref=inbox.at[d],
            send_sem=send.at[d], recv_sem=arrive.at[d],
            device_id={"ctx": peer}, device_id_type=mesh_ids,
        )

    def result(d):
        return pltpu.make_async_remote_copy(
            src_ref=out.at[mine], dst_ref=out.at[mine],
            send_sem=share.at[d], recv_sem=gather.at[d],
            device_id={"ctx": peer_of(d)}, device_id_type=mesh_ids,
        )

    def landed(d):
        sender = lax.rem(me - d - 1 + count, count)
        theirs = pl.ds(sender * chunk, chunk)
        return pltpu.make_async_remote_copy(
            src_ref=out.at[mine], dst_ref=out.at[theirs],
            send_sem=share.at[d], recv_sem=gather.at[d],
            device_id={"ctx": peer_of(d)}, device_id_type=mesh_ids,
        )

    def loop(action):
        def body(d, _):
            action(d)
            return 0

        lax.fori_loop(0, count - 1, body, 0)

    loop(lambda d: piece(d).start())
    out[mine] = own[mine]

    def collect(d):
        piece(d).wait_recv()
        out[mine] = out[mine] + inbox[d]

    loop(collect)
    loop(lambda d: result(d).start())
    loop(lambda d: piece(d).wait_send())
    loop(lambda d: landed(d).wait_recv())
    loop(lambda d: result(d).wait_send())


def on_device(section_out, stash, grad_out, taps, residues, decays, doc_lengths):
    stashed = stash[0]
    rows, width = stashed.shape
    modes, filters = residues.shape[1:]
    branches, taps_count = taps.shape[1:3]
    group = width // filters
    blocks = width // BLOCK
    ctx_size = lax.axis_size("ctx")
    pipe_size = lax.axis_size("pipe")
    span = rows * ctx_size // 16 // rows + 1
    depth = (span - 1).bit_length()

    smem = pl.BlockSpec(memory_space=pltpu.SMEM)
    anywhere = pl.BlockSpec(memory_space=pl.ANY)
    tokens = pl.BlockSpec((rows, BLOCK), lambda b: (0, b))
    edge = pl.BlockSpec((8, BLOCK), lambda b: (0, b))

    def major(count):
        return pl.BlockSpec((None, count * SUB, LANES), lambda b: (b, 0, 0))

    def shaped(count):
        return jax.ShapeDtypeStruct((blocks, count * SUB, LANES), F32)

    def scratch(count):
        return pltpu.VMEM((count * SUB, LANES), F32)

    def cost(ops, count):
        return pl.CostEstimate(flops=ops * rows * width, bytes_accessed=4 * count * rows * width, transcendentals=0)

    wide = jax.ShapeDtypeStruct((rows, width), jnp.bfloat16)
    tail = [
        pl.BlockSpec((branches * taps_count, SUB, LANES), lambda b: (0, b, 0)),
        major(2 * modes),
        major(modes),
    ]
    rim_old = from_behind(stashed[rows - 8 :], "ctx", 1)
    rim_new = lax.ppermute(
        section_out[0, rows - 8 :],
        ("ctx", "pipe"),
        [
            (c * pipe_size + p, (c + 1) * pipe_size + (p + 1) % pipe_size)
            for c in range(ctx_size - 1)
            for p in range(pipe_size)
        ],
    )
    upstream = passed_along(grad_out, "pipe", -1)[0]
    incoming = passed_along(section_out, "pipe", 1)[0]
    whole = pl.BlockSpec(memory_space=pltpu.VMEM)
    notes = jax.ShapeDtypeStruct((HEAD + rows + 16,), jnp.int32)
    meta_new, meta_old, dtab, resid = pl.pallas_call(
        functools.partial(prepare_kernel, rows, blocks),
        in_specs=[smem, whole, whole],
        out_specs=[smem, smem, whole, whole],
        out_shape=[notes, notes, shaped(2 * modes), shaped(modes)],
        name="prepare",
    )(doc_lengths, decays[0], residues[0])
    tapped = taps[0].reshape(branches * taps_count, blocks * SUB, LANES)
    through_new, through_old = meta_new[6].astype(F32), meta_old[6].astype(F32)
    decay = dtab[:, modes * SUB :]

    def link(earlier, later):
        return (earlier[0] * later[0], later[0] * earlier[1] + later[1])

    def nearby(through, summary, sign):
        if depth == 0:
            return from_behind(summary, "ctx", sign)
        current = (through * decay**rows, summary)
        for j in range(depth + 1):
            reach = 1 if j == 0 else 2 ** (j - 1)
            moved = from_behind(current, "ctx", sign * reach)
            current = moved if j == 0 else link(moved, current)
        return current[1]

    xs, qs, ks, vs, gs, longs, end_old = pl.pallas_call(
        functools.partial(forward_kernel, rows, modes, taps_count, full=True),
        grid=(blocks,),
        in_specs=[smem, tokens, edge] + tail,
        out_specs=[major(rows + 8)] + [major(rows)] * 5 + [major(modes)],
        out_shape=[shaped(rows + 8)] + [shaped(rows)] * 5 + [shaped(modes)],
        cost_estimate=cost(110, 7),
        name="forward_old",
    )(meta_old, stashed, rim_old, tapped, dtab, resid)
    state_old = nearby(through_old, end_old, 1)

    qn, gn, longn, end_new = pl.pallas_call(
        functools.partial(forward_kernel, rows, modes, taps_count, full=False),
        grid=(blocks,),
        in_specs=[smem, tokens, edge] + tail,
        out_specs=[major(rows)] * 3 + [major(modes)],
        out_shape=[shaped(rows)] * 3 + [shaped(modes)],
        scratch_shapes=[scratch(rows + 8)],
        cost_estimate=cost(110, 4),
        name="forward_new",
    )(meta_new, incoming, rim_new, tapped, dtab, resid)
    state_new = nearby(through_new, end_new, 1)

    dq, dl, dg, begin, sums, rim = pl.pallas_call(
        functools.partial(backward_kernel, rows, modes),
        grid=(blocks,),
        in_specs=[smem, tokens] + [major(rows)] * 5 + [major(modes)] + tail[1:] + [anywhere],
        out_specs=[major(rows)] * 3 + [major(modes)] * 2 + [major(24)],
        out_shape=[shaped(rows)] * 3 + [shaped(modes)] * 2 + [shaped(24)],
        scratch_shapes=[scratch(rows)],
        cost_estimate=cost(120, 8),
        name="backward_main",
    )(meta_old, upstream, qs, ks, vs, gs, longs, state_old, dtab, resid, end_new)
    later = nearby(through_old, begin, -1)
    if depth > 0:
        spread = (blocks, modes, SUB, LANES)
        extra = jnp.stack(
            [jnp.sum((resid * later * decay ** (rows - r)).reshape(spread), axis=1) for r in range(8)], axis=1
        ).reshape(blocks, 8 * SUB, LANES) * through_old
        head = 8 * SUB
        rim = rim + jnp.concatenate(
            [jnp.zeros_like(extra), extra * vs[:, :head], extra * ks[:, :head]], axis=1
        )
    rim_in = from_behind(rim, "ctx", -1)

    mixed = pl.pallas_call(
        functools.partial(mixed_kernel, rows, modes),
        grid=(blocks,),
        in_specs=[smem] + [major(rows)] * 3 + [major(modes)] + tail[1:],
        out_specs=tokens,
        out_shape=wide,
        scratch_shapes=[scratch(rows)],
        cost_estimate=cost(30, 4),
        name="mixed",
    )(meta_new, qn, gn, longn, state_new, dtab, resid)

    slots = branches * taps_count + 1
    back, partial = pl.pallas_call(
        functools.partial(finish_kernel, rows, modes, taps_count, group),
        grid=(blocks,),
        in_specs=[smem, major(rows + 8)] + [major(rows)] * 6 + [major(24)] + [major(modes)] * 2 + tail + [anywhere],
        out_specs=[tokens, pl.BlockSpec((slots, SUB, LANES), lambda b: (0, b, 0))],
        out_shape=[wide, jax.ShapeDtypeStruct((slots, blocks * SUB, LANES), F32)],
        scratch_shapes=[scratch(rows)] * 3,
        cost_estimate=cost(150, 8),
        name="finish",
    )(meta_old, xs, ks, vs, gs, dq, dl, dg, rim_in, later, sums, tapped, dtab, resid, mixed)

    tiles = slots * blocks
    chunk = -(-tiles // ctx_size)
    partial = partial.reshape(tiles, SUB, LANES)
    if chunk * ctx_size > tiles:
        partial = jnp.pad(partial, ((0, chunk * ctx_size - tiles), (0, 0), (0, 0)))
    hops = ctx_size - 1
    summed = pl.pallas_call(
        functools.partial(sum_kernel, ctx_size, chunk),
        in_specs=[whole],
        out_specs=whole,
        out_shape=jax.ShapeDtypeStruct(partial.shape, F32),
        scratch_shapes=[pltpu.VMEM((hops, chunk, SUB, LANES), F32)] + [pltpu.SemaphoreType.DMA((hops,))] * 4,
        compiler_params=pltpu.CompilerParams(collective_id=0, has_side_effects=True),
        name="window_sum",
    )(partial)
    cut = branches * taps_count * blocks
    tap_term = summed[:cut].reshape(branches, taps_count, width)
    filter_term = summed[cut:tiles].reshape(blocks, SUB, modes, LANES // group)
    filter_term = filter_term.transpose(2, 0, 1, 3).reshape(modes, filters)
    return (mixed[None], back[None], filter_term[None], tap_term[None])


def solution(mesh):
    in_specs = (
        P("pipe", "ctx", None),
        P("pipe", "ctx", None),
        P("pipe", "ctx", None),
        P("pipe", None, None, None),
        P("pipe", None, None),
        P("pipe", None, None),
        P(),
    )
    out_specs = (
        P("pipe", "ctx", None),
        P("pipe", "ctx", None),
        P("pipe", None, None),
        P("pipe", None, None, None),
    )
    return jax.shard_map(
        on_device, mesh=mesh, in_specs=in_specs, out_specs=out_specs, check_vma=False
    )
```

```python
import functools
import jax
import jax.numpy as jnp
from jax import lax
from jax.experimental import pallas as pl
from jax.experimental.pallas import tpu as pltpu
from jax.sharding import PartitionSpec as P


F32 = jnp.float32
SHIFT = 2
UNROLL = 1 << SHIFT
LANES = 128
SUB = 8
BLOCK = LANES * SUB


def from_behind(value, axis, steps):
    count = lax.axis_size(axis)
    initial, last = (max(0, -steps), min(count, count - steps))
    return lax.ppermute(value, axis, [(source, source + steps) for source in range(initial, last)])


def passed_along(array, axis, by):
    count = lax.axis_size(axis)
    return lax.ppermute(array, axis, [(i, (i + by) % count) for i in range(count)])


HEAD = 8


def at(ref, t):
    return ref[pl.ds(pl.multiple_of(t * SUB, SUB), SUB), :]


def put(ref, t, value):
    ref[pl.ds(pl.multiple_of(t * SUB, SUB), SUB), :] = value


def scatter_rows(src, dst, rows, offset):
    def body(g, _):
        for c in range(SUB):
            tile = src[pl.ds(pl.multiple_of(g * 16, 16), 16), c * LANES : (c + 1) * LANES].astype(F32)
            for h in range(2):
                dst[pl.ds((offset + g * 16 + h * 8) * SUB + c, 8, stride=SUB), :] = tile[h * 8 : h * 8 + 8]
        return 0

    lax.fori_loop(0, rows // 16, body, 0)


def gather_rows(src, dst, rows):
    def body(g, _):
        for c in range(SUB):
            halves = [src[pl.ds((g * 16 + h * 8) * SUB + c, 8, stride=SUB), :] for h in range(2)]
            dst[pl.ds(pl.multiple_of(g * 16, 16), 16), c * LANES : (c + 1) * LANES] = jnp.concatenate(
                halves, axis=0
            ).astype(dst.dtype)
        return 0

    lax.fori_loop(0, rows // 16, body, 0)


def total_of(parts):
    while len(parts) > 1:
        parts = [a + b for a, b in zip(parts[::2], parts[1::2])] + ([parts[-1]] if len(parts) % 2 else [])
    return parts[0]


def decayed(dtab, flag, states, value):
    modes = len(states)
    return [
        states[m] * dtab[pl.ds(pl.multiple_of(flag * (modes * SUB) + m * SUB, SUB), SUB), :] + value
        for m in range(modes)
    ]


def load_states(ref, modes):
    return tuple(at(ref, m) for m in range(modes))


def scan_forward(meta, source, dtab, resid, lo, hi, init, emit):
    modes = len(init)

    def body(g, states):
        states = list(states)
        for u in range(UNROLL):
            t = g * UNROLL + u
            states = decayed(dtab, meta[HEAD + t], states, at(source, t))
            emit(t, total_of([at(resid, m) * states[m] for m in range(modes)]))
        return tuple(states)

    return lax.fori_loop(lo, hi, body, init)


def scan_backward(meta, cotan, source, dtab, resid, lo, hi, init, totals, weight, emit):
    modes = len(init)

    def body(i, carry):
        states, sums = list(carry[0]), list(carry[1])
        g = hi - 1 - i
        for u in reversed(range(UNROLL)):
            t = g * UNROLL + u
            states = decayed(dtab, meta[HEAD + t + 1], states, at(cotan, t))
            emit(t, total_of([at(resid, m) * states[m] for m in range(modes)]))
            value = at(source, t) * weight(t)
            sums = [sums[m] + value * states[m] for m in range(modes)]
        return tuple(states), tuple(sums)

    return lax.fori_loop(0, hi - lo, body, (init, totals))


def forward_kernel(rows, modes, taps_count, meta, x, rim, taps, dtab, resid, *outs, full):
    if full:
        xs, qs, ks, vs, gs, longs, end = outs
    else:
        qs, gs, longs, end, xs = outs
    for c in range(SUB):
        xs[pl.ds(c, 8, stride=SUB), :] = rim[:, c * LANES : (c + 1) * LANES].astype(F32)
    scatter_rows(x, xs, rows, 8)
    age = meta[5]
    window = tuple(
        at(xs, 8 - j) * jnp.where(age >= j, 1.0, 0.0).astype(F32) for j in range(1, taps_count)
    )

    def feats(g, window):
        window = list(window)
        for u in range(2):
            t = g * 2 + u
            keep = meta[HEAD + t].astype(F32)
            now = at(xs, t + 8)
            seen = [now] + [w * keep for w in window]
            q, k, v = [
                total_of([taps[i * taps_count + j] * seen[j] for j in range(taps_count)])
                for i in range(3)
            ]
            put(qs, t, q)
            put(gs, t, k * v)
            if full:
                put(ks, t, k)
                put(vs, t, v)
            window = seen[:-1]
        return tuple(window)

    lax.fori_loop(0, rows // 2, feats, window)
    init = tuple(jnp.zeros((SUB, LANES), F32) for _ in range(modes))
    states = scan_forward(
        meta, gs, dtab, resid, meta[1], rows // UNROLL, init, lambda t, y: put(longs, t, y)
    )
    for m in range(modes):
        put(end, m, states[m])


def mixed_kernel(rows, modes, meta, qs, gs, longs, state, dtab, resid, out, scratch):
    def product(g, _):
        for u in range(8):
            t = g * 8 + u
            put(scratch, t, at(qs, t) * at(longs, t))
        return 0

    lax.fori_loop(0, rows // 8, product, 0)
    scan_forward(
        meta, gs, dtab, resid, 0, meta[0], load_states(state, modes),
        lambda t, y: put(scratch, t, y * at(qs, t)),
    )
    gather_rows(scratch, out, rows)


def backward_kernel(
    rows, modes, meta, up, qs, ks, vs, gs, longs, state, dtab, resid, after,
    dq, dl, dg, turn, sums, ups,
):
    scatter_rows(up, ups, rows, 0)

    def product(g, _):
        for u in range(8):
            t = g * 8 + u
            value = at(ups, t)
            put(dq, t, value * at(longs, t))
            put(dl, t, value * at(qs, t))
            put(dg, t, jnp.zeros((SUB, LANES), F32))
        return 0

    lax.fori_loop(0, rows // 8, product, 0)
    scan_forward(
        meta, gs, dtab, resid, 0, meta[0], load_states(state, modes),
        lambda t, y: put(dq, t, y * at(ups, t)),
    )
    zeros = tuple(jnp.zeros((SUB, LANES), F32) for _ in range(modes))
    last = meta[4]
    states, totals = scan_backward(
        meta, dl, gs, dtab, resid, 0, meta[2], zeros, zeros,
        lambda t: jnp.where(t < last, 1.0, 0.0).astype(F32),
        lambda t, y: put(dg, t, y),
    )
    for m in range(modes):
        put(turn, m, states[m])
        put(sums, m, totals[m])
    for t in range(8):
        value = at(dg, t)
        put(turn, modes + t, at(dq, t))
        put(turn, modes + 8 + t, value * at(vs, t))
        put(turn, modes + 16 + t, value * at(ks, t))


def finish_kernel(
    rows, modes, taps_count, group, meta, xs, ks, vs, gs, dq, dl, dg, turn, sums, taps, dtab, resid, after,
    out, tap_out, dks, dvs, backs,
):
    def copy(g, _):
        for u in range(8):
            put(dks, g * 8 + u, at(dg, g * 8 + u))
        return 0

    lax.fori_loop(0, rows // 8, copy, 0)
    last = meta[4]
    _, totals = scan_backward(
        meta, dl, gs, dtab, resid, meta[3], rows // UNROLL, load_states(turn, modes),
        load_states(sums, modes),
        lambda t: jnp.where(t >= last, 1.0, 0.0).astype(F32),
        lambda t, y: put(dks, t, y),
    )
    lane = lax.broadcasted_iota(jnp.int32, (SUB, LANES), 1)
    groups = LANES // group
    filter_tile = jnp.zeros((SUB, LANES), F32)
    for m in range(modes):
        part, step = totals[m], 1
        while step < group:
            part = part + pltpu.roll(part, LANES - step, 1)
            step *= 2
        moved = jnp.take_along_axis(part, lane % groups * group, axis=1)
        filter_tile = jnp.where(lane // groups == m, moved, filter_tile)
    tap_out[3 * taps_count] = filter_tile

    def spread(pending, grads, keep):
        parts = [
            total_of([taps[i * taps_count + j] * grads[i] for i in range(3)])
            for j in range(taps_count)
        ]
        done = pending[0] + parts[0]
        later = list(pending[1:]) + [None]
        return done, tuple(
            ((parts[k + 1] + later[k]) if later[k] is not None else parts[k + 1]) * keep
            for k in range(taps_count - 1)
        )

    pending = tuple(jnp.zeros((SUB, LANES), F32) for _ in range(taps_count - 1))
    for r in reversed(range(taps_count - 1)):
        grads = [at(turn, modes + i * 8 + r) for i in range(3)]
        _, pending = spread(pending, grads, meta[HEAD + rows + r].astype(F32))

    def descend(i, pending):
        g = rows // 2 - 1 - i
        for u in reversed(range(2)):
            t = g * 2 + u
            gated = at(dks, t)
            dk = gated * at(vs, t)
            dv = gated * at(ks, t)
            put(dks, t, dk)
            put(dvs, t, dv)
            done, pending = spread(pending, [at(dq, t), dk, dv], meta[HEAD + t].astype(F32))
            put(backs, t, done)
        return pending

    lax.fori_loop(0, rows // 2, descend, pending)
    gather_rows(backs, out, rows)
    age = meta[5]
    window = tuple(
        at(xs, 8 - j) * jnp.where(age >= j, 1.0, 0.0).astype(F32) for j in range(1, taps_count)
    )
    zeros = tuple(jnp.zeros((SUB, LANES), F32) for _ in range(3 * taps_count))

    def ascend(g, carry):
        window, acc = list(carry[0]), list(carry[1])
        for u in range(2):
            t = g * 2 + u
            keep = meta[HEAD + t].astype(F32)
            seen = [at(xs, t + 8)] + [w * keep for w in window]
            grads = [at(dq, t), at(dks, t), at(dvs, t)]
            acc = [
                acc[i * taps_count + j] + grads[i] * seen[j]
                for i in range(3)
                for j in range(taps_count)
            ]
            window = seen[:-1]
        return tuple(window), tuple(acc)

    _, acc = lax.fori_loop(0, rows // 2, ascend, (window, zeros))
    for n in range(3 * taps_count):
        tap_out[n] = acc[n]


def prepare_kernel(rows, blocks, lengths, rates, resids, meta_new, meta_old, dtab, resid):
    base = lax.axis_index("ctx") * rows
    reach = rows + 16
    for which, meta in enumerate((meta_new, meta_old)):

        def fill(i, _):
            for u in range(8):
                meta[i * 8 + u] = 1
            return 0

        lax.fori_loop(0, (HEAD + reach) // 8, fill, 0)

        def document(i, carry):
            offset, first, last, begin = carry
            inside = jnp.logical_and(offset >= 0, offset < reach)
            meta[jnp.where(inside, HEAD + offset, 7)] = 0
            first = jnp.where(offset >= 0, jnp.minimum(first, offset), first)
            last = jnp.where(jnp.logical_and(offset >= 0, offset < rows), offset, last)
            begin = jnp.where(offset <= 0, offset, begin)
            return offset + lengths[which, i], first, last, begin

        start = (-base, jnp.int32(rows), jnp.int32(-1), jnp.int32(0))
        _, first, last, begin = lax.fori_loop(0, lengths.shape[1], document, start)
        through = first == rows
        meta[0] = lax.shift_right_logical(first + (UNROLL - 1), SHIFT)
        meta[1] = jnp.where(through, 0, lax.shift_right_logical(first, SHIFT))
        meta[2] = jnp.where(through, rows // UNROLL, lax.shift_right_logical(last + (UNROLL - 1), SHIFT))
        meta[3] = lax.shift_right_logical(jnp.maximum(last, 0), SHIFT)
        meta[4] = last
        meta[5] = -begin
        meta[6] = jnp.where(through, 1, 0)
    modes, filters = rates.shape
    group = blocks * BLOCK // filters
    lane = lax.broadcasted_iota(jnp.int32, (modes, LANES), 1) // group
    zeros = jnp.zeros((modes * SUB, LANES), F32)
    for b in range(blocks):
        dtab[b, 0 : modes * SUB, :] = zeros
        for c in range(SUB):
            low = (b * SUB + c) * (LANES // group)
            tile, place = low // LANES * LANES, low % LANES
            for source, target, offset in ((rates, dtab, modes * SUB), (resids, resid, 0)):
                wide = jnp.take_along_axis(source[:, tile : tile + LANES], lane + place, axis=1)
                if target is dtab:
                    wide = jnp.exp(-wide)
                for h in range(0, modes, 8):
                    target[b, pl.ds(offset + h * SUB + c, 8, stride=SUB), :] = wide[h : h + 8]


def sum_kernel(count, chunk, own, out, inbox, send, arrive, share, gather):
    me = lax.axis_index("ctx")
    mine = pl.ds(me * chunk, chunk)
    mesh_ids = pl.DeviceIdType.MESH

    def peer_of(d):
        return lax.rem(me + d + 1, count)

    barrier = pltpu.get_barrier_semaphore()

    def greet(d, _):
        pl.semaphore_signal(barrier, inc=1, device_id={"ctx": peer_of(d)}, device_id_type=mesh_ids)
        return 0

    lax.fori_loop(0, count - 1, greet, 0)
    pl.semaphore_wait(barrier, count - 1)

    def piece(d):
        peer = peer_of(d)
        return pltpu.make_async_remote_copy(
            src_ref=own.at[pl.ds(peer * chunk, chunk)], dst_ref=inbox.at[d],
            send_sem=send.at[d], recv_sem=arrive.at[d],
            device_id={"ctx": peer}, device_id_type=mesh_ids,
        )

    def result(d):
        return pltpu.make_async_remote_copy(
            src_ref=out.at[mine], dst_ref=out.at[mine],
            send_sem=share.at[d], recv_sem=gather.at[d],
            device_id={"ctx": peer_of(d)}, device_id_type=mesh_ids,
        )

    def landed(d):
        sender = lax.rem(me - d - 1 + count, count)
        theirs = pl.ds(sender * chunk, chunk)
        return pltpu.make_async_remote_copy(
            src_ref=out.at[mine], dst_ref=out.at[theirs],
            send_sem=share.at[d], recv_sem=gather.at[d],
            device_id={"ctx": peer_of(d)}, device_id_type=mesh_ids,
        )

    def loop(action):
        def body(d, _):
            action(d)
            return 0

        lax.fori_loop(0, count - 1, body, 0)

    loop(lambda d: piece(d).start())
    out[mine] = own[mine]

    def collect(d):
        piece(d).wait_recv()
        out[mine] = out[mine] + inbox[d]

    loop(collect)
    loop(lambda d: result(d).start())
    loop(lambda d: piece(d).wait_send())
    loop(lambda d: landed(d).wait_recv())
    loop(lambda d: result(d).wait_send())


def on_device(section_out, stash, grad_out, taps, residues, decays, doc_lengths):
    stashed = stash[0]
    rows, width = stashed.shape
    modes, filters = residues.shape[1:]
    branches, taps_count = taps.shape[1:3]
    group = width // filters
    blocks = width // BLOCK
    ctx_size = lax.axis_size("ctx")
    pipe_size = lax.axis_size("pipe")
    span = rows * ctx_size // 16 // rows + 1
    depth = (span - 1).bit_length()

    smem = pl.BlockSpec(memory_space=pltpu.SMEM)
    anywhere = pl.BlockSpec(memory_space=pl.ANY)
    tokens = pl.BlockSpec((rows, BLOCK), lambda b: (0, b))
    edge = pl.BlockSpec((8, BLOCK), lambda b: (0, b))

    def major(count):
        return pl.BlockSpec((None, count * SUB, LANES), lambda b: (b, 0, 0))

    def shaped(count):
        return jax.ShapeDtypeStruct((blocks, count * SUB, LANES), F32)

    def scratch(count):
        return pltpu.VMEM((count * SUB, LANES), F32)

    def cost(ops, count):
        return pl.CostEstimate(flops=ops * rows * width, bytes_accessed=4 * count * rows * width, transcendentals=0)

    wide = jax.ShapeDtypeStruct((rows, width), jnp.bfloat16)
    tail = [
        pl.BlockSpec((branches * taps_count, SUB, LANES), lambda b: (0, b, 0)),
        major(2 * modes),
        major(modes),
    ]
    rim_old = from_behind(stashed[rows - 8 :], "ctx", 1)
    rim_new = lax.ppermute(
        section_out[0, rows - 8 :],
        ("ctx", "pipe"),
        [
            (c * pipe_size + p, (c + 1) * pipe_size + (p + 1) % pipe_size)
            for c in range(ctx_size - 1)
            for p in range(pipe_size)
        ],
    )
    upstream = passed_along(grad_out, "pipe", -1)[0]
    incoming = passed_along(section_out, "pipe", 1)[0]
    whole = pl.BlockSpec(memory_space=pltpu.VMEM)
    notes = jax.ShapeDtypeStruct((HEAD + rows + 16,), jnp.int32)
    meta_new, meta_old, dtab, resid = pl.pallas_call(
        functools.partial(prepare_kernel, rows, blocks),
        in_specs=[smem, whole, whole],
        out_specs=[smem, smem, whole, whole],
        out_shape=[notes, notes, shaped(2 * modes), shaped(modes)],
        name="prepare",
    )(doc_lengths, decays[0], residues[0])
    tapped = taps[0].reshape(branches * taps_count, blocks * SUB, LANES)
    through_new, through_old = meta_new[6].astype(F32), meta_old[6].astype(F32)
    decay = dtab[:, modes * SUB :]

    def link(earlier, later):
        return (earlier[0] * later[0], later[0] * earlier[1] + later[1])

    def nearby(through, summary, sign):
        if depth == 0:
            return from_behind(summary, "ctx", sign)
        current = (through * decay**rows, summary)
        for j in range(depth + 1):
            reach = 1 if j == 0 else 2 ** (j - 1)
            moved = from_behind(current, "ctx", sign * reach)
            current = moved if j == 0 else link(moved, current)
        return current[1]

    xs, qs, ks, vs, gs, longs, end_old = pl.pallas_call(
        functools.partial(forward_kernel, rows, modes, taps_count, full=True),
        grid=(blocks,),
        in_specs=[smem, tokens, edge] + tail,
        out_specs=[major(rows + 8)] + [major(rows)] * 5 + [major(modes)],
        out_shape=[shaped(rows + 8)] + [shaped(rows)] * 5 + [shaped(modes)],
        cost_estimate=cost(110, 7),
        name="forward_old",
    )(meta_old, stashed, rim_old, tapped, dtab, resid)
    state_old = nearby(through_old, end_old, 1)

    qn, gn, longn, end_new = pl.pallas_call(
        functools.partial(forward_kernel, rows, modes, taps_count, full=False),
        grid=(blocks,),
        in_specs=[smem, tokens, edge] + tail,
        out_specs=[major(rows)] * 3 + [major(modes)],
        out_shape=[shaped(rows)] * 3 + [shaped(modes)],
        scratch_shapes=[scratch(rows + 8)],
        cost_estimate=cost(110, 4),
        name="forward_new",
    )(meta_new, incoming, rim_new, tapped, dtab, resid)
    state_new = nearby(through_new, end_new, 1)

    dq, dl, dg, turn, sums = pl.pallas_call(
        functools.partial(backward_kernel, rows, modes),
        grid=(blocks,),
        in_specs=[smem, tokens] + [major(rows)] * 5 + [major(modes)] + tail[1:] + [anywhere],
        out_specs=[major(rows)] * 3 + [major(modes + 24), major(modes)],
        out_shape=[shaped(rows)] * 3 + [shaped(modes + 24), shaped(modes)],
        scratch_shapes=[scratch(rows)],
        cost_estimate=cost(120, 8),
        name="backward_main",
    )(meta_old, upstream, qs, ks, vs, gs, longs, state_old, dtab, resid, state_new)
    if depth == 0:
        turn_in = from_behind(turn, "ctx", -1)
    else:
        later = nearby(through_old, turn[:, : modes * SUB], -1)
        rim = turn[:, modes * SUB :]
        spread = (blocks, modes, SUB, LANES)
        extra = jnp.stack(
            [jnp.sum((resid * later * decay ** (rows - r)).reshape(spread), axis=1) for r in range(8)], axis=1
        ).reshape(blocks, 8 * SUB, LANES) * through_old
        head = 8 * SUB
        rim = rim + jnp.concatenate(
            [jnp.zeros_like(extra), extra * vs[:, :head], extra * ks[:, :head]], axis=1
        )
        turn_in = jnp.concatenate([later, from_behind(rim, "ctx", -1)], axis=1)

    mixed = pl.pallas_call(
        functools.partial(mixed_kernel, rows, modes),
        grid=(blocks,),
        in_specs=[smem] + [major(rows)] * 3 + [major(modes)] + tail[1:],
        out_specs=tokens,
        out_shape=wide,
        scratch_shapes=[scratch(rows)],
        cost_estimate=cost(30, 4),
        name="mixed",
    )(meta_new, qn, gn, longn, state_new, dtab, resid)

    slots = branches * taps_count + 1
    back, partial = pl.pallas_call(
        functools.partial(finish_kernel, rows, modes, taps_count, group),
        grid=(blocks,),
        in_specs=[smem, major(rows + 8)] + [major(rows)] * 6 + [major(modes + 24), major(modes)] + tail + [anywhere],
        out_specs=[tokens, pl.BlockSpec((slots, SUB, LANES), lambda b: (0, b, 0))],
        out_shape=[wide, jax.ShapeDtypeStruct((slots, blocks * SUB, LANES), F32)],
        scratch_shapes=[scratch(rows)] * 3,
        cost_estimate=cost(150, 8),
        name="finish",
    )(meta_old, xs, ks, vs, gs, dq, dl, dg, turn_in, sums, tapped, dtab, resid, mixed)

    tiles = slots * blocks
    chunk = -(-tiles // ctx_size)
    partial = partial.reshape(tiles, SUB, LANES)
    if chunk * ctx_size > tiles:
        partial = jnp.pad(partial, ((0, chunk * ctx_size - tiles), (0, 0), (0, 0)))
    hops = ctx_size - 1
    summed = pl.pallas_call(
        functools.partial(sum_kernel, ctx_size, chunk),
        in_specs=[whole],
        out_specs=whole,
        out_shape=jax.ShapeDtypeStruct(partial.shape, F32),
        scratch_shapes=[pltpu.VMEM((hops, chunk, SUB, LANES), F32)] + [pltpu.SemaphoreType.DMA((hops,))] * 4,
        compiler_params=pltpu.CompilerParams(collective_id=0, has_side_effects=True),
        name="window_sum",
    )(partial)
    cut = branches * taps_count * blocks
    tap_term = summed[:cut].reshape(branches, taps_count, width)
    filter_term = summed[cut:tiles].reshape(blocks, SUB, modes, LANES // group)
    filter_term = filter_term.transpose(2, 0, 1, 3).reshape(modes, filters)
    return (mixed[None], back[None], filter_term[None], tap_term[None])


def solution(mesh):
    in_specs = (
        P("pipe", "ctx", None),
        P("pipe", "ctx", None),
        P("pipe", "ctx", None),
        P("pipe", None, None, None),
        P("pipe", None, None),
        P("pipe", None, None),
        P(),
    )
    out_specs = (
        P("pipe", "ctx", None),
        P("pipe", "ctx", None),
        P("pipe", None, None),
        P("pipe", None, None, None),
    )

    return jax.shard_map(
        on_device, mesh=mesh, in_specs=in_specs, out_specs=out_specs, check_vma=False
    )
```

```python
import functools
import jax
import jax.numpy as jnp
from jax import lax
from jax.experimental import pallas as pl
from jax.experimental.pallas import tpu as pltpu
from jax.sharding import PartitionSpec as P


F32 = jnp.float32
SHIFT = 3
UNROLL = 1 << SHIFT
LANES = 128
SUB = 8
BLOCK = LANES * SUB


def from_behind(value, axis, steps):
    count = lax.axis_size(axis)
    initial, last = (max(0, -steps), min(count, count - steps))
    return lax.ppermute(value, axis, [(source, source + steps) for source in range(initial, last)])


def passed_along(array, axis, by):
    count = lax.axis_size(axis)
    return lax.ppermute(array, axis, [(i, (i + by) % count) for i in range(count)])


HEAD = 8


def at(ref, t):
    return ref[pl.ds(pl.multiple_of(t * SUB, SUB), SUB), :]


def put(ref, t, value):
    ref[pl.ds(pl.multiple_of(t * SUB, SUB), SUB), :] = value


def scatter_rows(src, dst, rows, offset):
    def body(g, _):
        for c in range(SUB):
            tile = src[pl.ds(pl.multiple_of(g * 16, 16), 16), c * LANES : (c + 1) * LANES].astype(F32)
            for h in range(2):
                dst[pl.ds((offset + g * 16 + h * 8) * SUB + c, 8, stride=SUB), :] = tile[h * 8 : h * 8 + 8]
        return 0

    lax.fori_loop(0, rows // 16, body, 0)


def gather_rows(src, dst, rows):
    def body(g, _):
        for c in range(SUB):
            halves = [src[pl.ds((g * 16 + h * 8) * SUB + c, 8, stride=SUB), :] for h in range(2)]
            dst[pl.ds(pl.multiple_of(g * 16, 16), 16), c * LANES : (c + 1) * LANES] = jnp.concatenate(
                halves, axis=0
            ).astype(dst.dtype)
        return 0

    lax.fori_loop(0, rows // 16, body, 0)


def total_of(parts):
    while len(parts) > 1:
        parts = [a + b for a, b in zip(parts[::2], parts[1::2])] + ([parts[-1]] if len(parts) % 2 else [])
    return parts[0]


def decayed(dtab, flag, states, value):
    modes = len(states)
    return [
        states[m] * dtab[pl.ds(pl.multiple_of(flag * (modes * SUB) + m * SUB, SUB), SUB), :] + value
        for m in range(modes)
    ]


def load_states(ref, modes):
    return tuple(at(ref, m) for m in range(modes))


def scan_forward(meta, source, dtab, resid, lo, hi, init, emit):
    modes = len(init)

    def body(g, states):
        states = list(states)
        for u in range(UNROLL):
            t = g * UNROLL + u
            states = decayed(dtab, meta[HEAD + t], states, at(source, t))
            emit(t, total_of([at(resid, m) * states[m] for m in range(modes)]))
        return tuple(states)

    return lax.fori_loop(lo, hi, body, init)


def scan_backward(meta, cotan, source, dtab, resid, lo, hi, init, totals, weight, emit):
    modes = len(init)

    def body(i, carry):
        states, sums = list(carry[0]), list(carry[1])
        g = hi - 1 - i
        for u in reversed(range(UNROLL)):
            t = g * UNROLL + u
            states = decayed(dtab, meta[HEAD + t + 1], states, at(cotan, t))
            emit(t, total_of([at(resid, m) * states[m] for m in range(modes)]))
            value = at(source, t) * weight(t)
            sums = [sums[m] + value * states[m] for m in range(modes)]
        return tuple(states), tuple(sums)

    return lax.fori_loop(0, hi - lo, body, (init, totals))


def forward_kernel(rows, modes, taps_count, meta, x, rim, taps, dtab, resid, *outs, full):
    if full:
        xs, qs, ks, vs, gs, longs, end = outs
    else:
        qs, gs, longs, end, xs = outs
    for c in range(SUB):
        xs[pl.ds(c, 8, stride=SUB), :] = rim[:, c * LANES : (c + 1) * LANES].astype(F32)
    scatter_rows(x, xs, rows, 8)
    age = meta[5]
    window = tuple(
        at(xs, 8 - j) * jnp.where(age >= j, 1.0, 0.0).astype(F32) for j in range(1, taps_count)
    )

    def feats(g, window):
        window = list(window)
        for u in range(4):
            t = g * 4 + u
            keep = meta[HEAD + t].astype(F32)
            now = at(xs, t + 8)
            seen = [now] + [w * keep for w in window]
            q, k, v = [
                total_of([taps[i * taps_count + j] * seen[j] for j in range(taps_count)])
                for i in range(3)
            ]
            put(qs, t, q)
            put(gs, t, k * v)
            if full:
                put(ks, t, k)
                put(vs, t, v)
            window = seen[:-1]
        return tuple(window)

    lax.fori_loop(0, rows // 4, feats, window)
    init = tuple(jnp.zeros((SUB, LANES), F32) for _ in range(modes))
    states = scan_forward(
        meta, gs, dtab, resid, meta[1], rows // UNROLL, init, lambda t, y: put(longs, t, y)
    )
    for m in range(modes):
        put(end, m, states[m])


def mixed_kernel(rows, modes, meta, qs, gs, longs, state, dtab, resid, out, scratch):
    def product(g, _):
        for u in range(8):
            t = g * 8 + u
            put(scratch, t, at(qs, t) * at(longs, t))
        return 0

    lax.fori_loop(0, rows // 8, product, 0)
    scan_forward(
        meta, gs, dtab, resid, 0, meta[0], load_states(state, modes),
        lambda t, y: put(scratch, t, y * at(qs, t)),
    )
    gather_rows(scratch, out, rows)


def backward_kernel(
    rows, modes, meta, up, qs, ks, vs, gs, longs, state, dtab, resid, after,
    dq, dl, dg, turn, sums, ups,
):
    scatter_rows(up, ups, rows, 0)

    def product(g, _):
        for u in range(8):
            t = g * 8 + u
            value = at(ups, t)
            put(dq, t, value * at(longs, t))
            put(dl, t, value * at(qs, t))
            put(dg, t, jnp.zeros((SUB, LANES), F32))
        return 0

    lax.fori_loop(0, rows // 8, product, 0)
    scan_forward(
        meta, gs, dtab, resid, 0, meta[0], load_states(state, modes),
        lambda t, y: put(dq, t, y * at(ups, t)),
    )
    zeros = tuple(jnp.zeros((SUB, LANES), F32) for _ in range(modes))
    last = meta[4]
    states, totals = scan_backward(
        meta, dl, gs, dtab, resid, 0, meta[2], zeros, zeros,
        lambda t: jnp.where(t < last, 1.0, 0.0).astype(F32),
        lambda t, y: put(dg, t, y),
    )
    for m in range(modes):
        put(turn, m, states[m])
        put(sums, m, totals[m])
    halo = (turn.shape[0] // SUB - modes) // 3
    for t in range(halo):
        value = at(dg, t)
        put(turn, modes + t, at(dq, t))
        put(turn, modes + halo + t, value * at(vs, t))
        put(turn, modes + 2 * halo + t, value * at(ks, t))


def finish_kernel(
    rows, modes, taps_count, group, meta, xs, ks, vs, gs, dq, dl, dg, turn, sums, taps, dtab, resid, after,
    out, tap_out, dks, dvs, backs,
):
    def copy(g, _):
        for u in range(8):
            put(dks, g * 8 + u, at(dg, g * 8 + u))
        return 0

    lax.fori_loop(0, rows // 8, copy, 0)
    last = meta[4]
    _, totals = scan_backward(
        meta, dl, gs, dtab, resid, meta[3], rows // UNROLL, load_states(turn, modes),
        load_states(sums, modes),
        lambda t: jnp.where(t >= last, 1.0, 0.0).astype(F32),
        lambda t, y: put(dks, t, y),
    )
    lane = lax.broadcasted_iota(jnp.int32, (SUB, LANES), 1)
    groups = LANES // group
    filter_tile = jnp.zeros((SUB, LANES), F32)
    for m in range(modes):
        part, step = totals[m], 1
        while step < group:
            part = part + pltpu.roll(part, LANES - step, 1)
            step *= 2
        moved = jnp.take_along_axis(part, lane % groups * group, axis=1)
        filter_tile = jnp.where(lane // groups == m, moved, filter_tile)
    tap_out[3 * taps_count] = filter_tile

    def spread(pending, grads, keep):
        parts = [
            total_of([taps[i * taps_count + j] * grads[i] for i in range(3)])
            for j in range(taps_count)
        ]
        done = pending[0] + parts[0]
        later = list(pending[1:]) + [None]
        return done, tuple(
            ((parts[k + 1] + later[k]) if later[k] is not None else parts[k + 1]) * keep
            for k in range(taps_count - 1)
        )

    pending = tuple(jnp.zeros((SUB, LANES), F32) for _ in range(taps_count - 1))
    for r in reversed(range(taps_count - 1)):
        grads = [at(turn, modes + i * (taps_count - 1) + r) for i in range(3)]
        _, pending = spread(pending, grads, meta[HEAD + rows + r].astype(F32))

    def descend(i, pending):
        g = rows // 4 - 1 - i
        for u in reversed(range(4)):
            t = g * 4 + u
            gated = at(dks, t)
            dk = gated * at(vs, t)
            dv = gated * at(ks, t)
            put(dks, t, dk)
            put(dvs, t, dv)
            done, pending = spread(pending, [at(dq, t), dk, dv], meta[HEAD + t].astype(F32))
            put(backs, t, done)
        return pending

    lax.fori_loop(0, rows // 4, descend, pending)
    gather_rows(backs, out, rows)
    age = meta[5]
    window = tuple(
        at(xs, 8 - j) * jnp.where(age >= j, 1.0, 0.0).astype(F32) for j in range(1, taps_count)
    )
    zeros = tuple(jnp.zeros((SUB, LANES), F32) for _ in range(3 * taps_count))

    def ascend(g, carry):
        window, acc = list(carry[0]), list(carry[1])
        for u in range(4):
            t = g * 4 + u
            keep = meta[HEAD + t].astype(F32)
            seen = [at(xs, t + 8)] + [w * keep for w in window]
            grads = [at(dq, t), at(dks, t), at(dvs, t)]
            acc = [
                acc[i * taps_count + j] + grads[i] * seen[j]
                for i in range(3)
                for j in range(taps_count)
            ]
            window = seen[:-1]
        return tuple(window), tuple(acc)

    _, acc = lax.fori_loop(0, rows // 4, ascend, (window, zeros))
    for n in range(3 * taps_count):
        tap_out[n] = acc[n]


def prepare_kernel(rows, blocks, lengths, rates, resids, meta_new, meta_old, dtab, resid):
    base = lax.axis_index("ctx") * rows
    reach = rows + 16
    for which, meta in enumerate((meta_new, meta_old)):

        def fill(i, _):
            for u in range(8):
                meta[i * 8 + u] = 1
            return 0

        lax.fori_loop(0, (HEAD + reach) // 8, fill, 0)

        def document(i, carry):
            offset, first, last, begin = carry
            inside = jnp.logical_and(offset >= 0, offset < reach)
            meta[jnp.where(inside, HEAD + offset, 7)] = 0
            first = jnp.where(offset >= 0, jnp.minimum(first, offset), first)
            last = jnp.where(jnp.logical_and(offset >= 0, offset < rows), offset, last)
            begin = jnp.where(offset <= 0, offset, begin)
            return offset + lengths[which, i], first, last, begin

        start = (-base, jnp.int32(rows), jnp.int32(-1), jnp.int32(0))
        _, first, last, begin = lax.fori_loop(0, lengths.shape[1], document, start)
        through = first == rows
        meta[0] = lax.shift_right_logical(first + (UNROLL - 1), SHIFT)
        meta[1] = jnp.where(through, 0, lax.shift_right_logical(first, SHIFT))
        meta[2] = jnp.where(through, rows // UNROLL, lax.shift_right_logical(last + (UNROLL - 1), SHIFT))
        meta[3] = lax.shift_right_logical(jnp.maximum(last, 0), SHIFT)
        meta[4] = last
        meta[5] = -begin
        meta[6] = jnp.where(through, 1, 0)
    modes, filters = rates.shape
    group = blocks * BLOCK // filters
    lane = lax.broadcasted_iota(jnp.int32, (modes, LANES), 1) // group
    zeros = jnp.zeros((modes * SUB, LANES), F32)
    for b in range(blocks):
        dtab[b, 0 : modes * SUB, :] = zeros
        for c in range(SUB):
            low = (b * SUB + c) * (LANES // group)
            tile, place = low // LANES * LANES, low % LANES
            for source, target, offset in ((rates, dtab, modes * SUB), (resids, resid, 0)):
                wide = jnp.take_along_axis(source[:, tile : tile + LANES], lane + place, axis=1)
                if target is dtab:
                    wide = jnp.exp(-wide)
                for h in range(0, modes, 8):
                    target[b, pl.ds(offset + h * SUB + c, 8, stride=SUB), :] = wide[h : h + 8]


def sum_kernel(count, chunk, own, out, inbox, send, arrive, share, gather):
    me = lax.axis_index("ctx")
    mine = pl.ds(me * chunk, chunk)
    mesh_ids = pl.DeviceIdType.MESH

    def peer_of(d):
        return lax.rem(me + d + 1, count)

    barrier = pltpu.get_barrier_semaphore()

    def greet(d, _):
        pl.semaphore_signal(barrier, inc=1, device_id={"ctx": peer_of(d)}, device_id_type=mesh_ids)
        return 0

    lax.fori_loop(0, count - 1, greet, 0)
    pl.semaphore_wait(barrier, count - 1)

    def piece(d):
        peer = peer_of(d)
        return pltpu.make_async_remote_copy(
            src_ref=own.at[pl.ds(peer * chunk, chunk)], dst_ref=inbox.at[d],
            send_sem=send.at[d], recv_sem=arrive.at[d],
            device_id={"ctx": peer}, device_id_type=mesh_ids,
        )

    def result(d):
        return pltpu.make_async_remote_copy(
            src_ref=out.at[mine], dst_ref=out.at[mine],
            send_sem=share.at[d], recv_sem=gather.at[d],
            device_id={"ctx": peer_of(d)}, device_id_type=mesh_ids,
        )

    def landed(d):
        sender = lax.rem(me - d - 1 + count, count)
        theirs = pl.ds(sender * chunk, chunk)
        return pltpu.make_async_remote_copy(
            src_ref=out.at[mine], dst_ref=out.at[theirs],
            send_sem=share.at[d], recv_sem=gather.at[d],
            device_id={"ctx": peer_of(d)}, device_id_type=mesh_ids,
        )

    def loop(action):
        def body(d, _):
            action(d)
            return 0

        lax.fori_loop(0, count - 1, body, 0)

    loop(lambda d: piece(d).start())
    out[mine] = own[mine]

    def collect(d):
        piece(d).wait_recv()
        out[mine] = out[mine] + inbox[d]

    loop(collect)
    loop(lambda d: result(d).start())
    loop(lambda d: piece(d).wait_send())
    loop(lambda d: landed(d).wait_recv())
    loop(lambda d: result(d).wait_send())


def on_device(section_out, stash, grad_out, taps, residues, decays, doc_lengths):
    stashed = stash[0]
    rows, width = stashed.shape
    modes, filters = residues.shape[1:]
    branches, taps_count = taps.shape[1:3]
    group = width // filters
    blocks = width // BLOCK
    ctx_size = lax.axis_size("ctx")
    pipe_size = lax.axis_size("pipe")
    span = rows * ctx_size // 16 // rows + 1
    depth = (span - 1).bit_length()

    smem = pl.BlockSpec(memory_space=pltpu.SMEM)
    anywhere = pl.BlockSpec(memory_space=pl.ANY)
    tokens = pl.BlockSpec((rows, BLOCK), lambda b: (0, b))
    edge = pl.BlockSpec((8, BLOCK), lambda b: (0, b))

    def major(count):
        return pl.BlockSpec((None, count * SUB, LANES), lambda b: (b, 0, 0))

    def shaped(count):
        return jax.ShapeDtypeStruct((blocks, count * SUB, LANES), F32)

    def scratch(count):
        return pltpu.VMEM((count * SUB, LANES), F32)

    def cost(ops, count):
        return pl.CostEstimate(flops=ops * rows * width, bytes_accessed=4 * count * rows * width, transcendentals=0)

    wide = jax.ShapeDtypeStruct((rows, width), jnp.bfloat16)
    tail = [
        pl.BlockSpec((branches * taps_count, SUB, LANES), lambda b: (0, b, 0)),
        major(2 * modes),
        major(modes),
    ]
    rim_old = from_behind(stashed[rows - 8 :], "ctx", 1)
    rim_new = lax.ppermute(
        section_out[0, rows - 8 :],
        ("ctx", "pipe"),
        [
            (c * pipe_size + p, (c + 1) * pipe_size + (p + 1) % pipe_size)
            for c in range(ctx_size - 1)
            for p in range(pipe_size)
        ],
    )
    upstream = passed_along(grad_out, "pipe", -1)[0]
    incoming = passed_along(section_out, "pipe", 1)[0]
    whole = pl.BlockSpec(memory_space=pltpu.VMEM)
    notes = jax.ShapeDtypeStruct((HEAD + rows + 16,), jnp.int32)
    meta_new, meta_old, dtab, resid = pl.pallas_call(
        functools.partial(prepare_kernel, rows, blocks),
        in_specs=[smem, whole, whole],
        out_specs=[smem, smem, whole, whole],
        out_shape=[notes, notes, shaped(2 * modes), shaped(modes)],
        name="prepare",
    )(doc_lengths, decays[0], residues[0])
    tapped = taps[0].reshape(branches * taps_count, blocks * SUB, LANES)
    through_new, through_old = meta_new[6].astype(F32), meta_old[6].astype(F32)
    decay = dtab[:, modes * SUB :]

    def link(earlier, later):
        return (earlier[0] * later[0], later[0] * earlier[1] + later[1])

    def nearby(through, summary, sign):
        if depth == 0:
            return from_behind(summary, "ctx", sign)
        current = (through * decay**rows, summary)
        for j in range(depth + 1):
            reach = 1 if j == 0 else 2 ** (j - 1)
            moved = from_behind(current, "ctx", sign * reach)
            current = moved if j == 0 else link(moved, current)
        return current[1]

    xs, qs, ks, vs, gs, longs, end_old = pl.pallas_call(
        functools.partial(forward_kernel, rows, modes, taps_count, full=True),
        grid=(blocks,),
        in_specs=[smem, tokens, edge] + tail,
        out_specs=[major(rows + 8)] + [major(rows)] * 5 + [major(modes)],
        out_shape=[shaped(rows + 8)] + [shaped(rows)] * 5 + [shaped(modes)],
        cost_estimate=cost(110, 7),
        name="forward_old",
    )(meta_old, stashed, rim_old, tapped, dtab, resid)
    state_old = nearby(through_old, end_old, 1)

    qn, gn, longn, end_new = pl.pallas_call(
        functools.partial(forward_kernel, rows, modes, taps_count, full=False),
        grid=(blocks,),
        in_specs=[smem, tokens, edge] + tail,
        out_specs=[major(rows)] * 3 + [major(modes)],
        out_shape=[shaped(rows)] * 3 + [shaped(modes)],
        scratch_shapes=[scratch(rows + 8)],
        cost_estimate=cost(110, 4),
        name="forward_new",
    )(meta_new, incoming, rim_new, tapped, dtab, resid)
    state_new = nearby(through_new, end_new, 1)

    dq, dl, dg, turn, sums = pl.pallas_call(
        functools.partial(backward_kernel, rows, modes),
        grid=(blocks,),
        in_specs=[smem, tokens] + [major(rows)] * 5 + [major(modes)] + tail[1:] + [anywhere],
        out_specs=[major(rows)] * 3 + [major(modes + 3 * (taps_count - 1)), major(modes)],
        out_shape=[shaped(rows)] * 3 + [shaped(modes + 3 * (taps_count - 1)), shaped(modes)],
        scratch_shapes=[scratch(rows)],
        cost_estimate=cost(120, 8),
        name="backward_main",
    )(meta_old, upstream, qs, ks, vs, gs, longs, state_old, dtab, resid, state_new)
    if depth == 0:
        turn_in = from_behind(turn, "ctx", -1)
    else:
        later = nearby(through_old, turn[:, : modes * SUB], -1)
        rim = turn[:, modes * SUB :]
        spread = (blocks, modes, SUB, LANES)
        extra = jnp.stack(
            [jnp.sum((resid * later * decay ** (rows - r)).reshape(spread), axis=1) for r in range(taps_count - 1)], axis=1
        ).reshape(blocks, (taps_count - 1) * SUB, LANES) * through_old
        head = (taps_count - 1) * SUB
        rim = rim + jnp.concatenate(
            [jnp.zeros_like(extra), extra * vs[:, :head], extra * ks[:, :head]], axis=1
        )
        turn_in = jnp.concatenate([later, from_behind(rim, "ctx", -1)], axis=1)

    mixed = pl.pallas_call(
        functools.partial(mixed_kernel, rows, modes),
        grid=(blocks,),
        in_specs=[smem] + [major(rows)] * 3 + [major(modes)] + tail[1:],
        out_specs=tokens,
        out_shape=wide,
        scratch_shapes=[scratch(rows)],
        cost_estimate=cost(30, 4),
        name="mixed",
    )(meta_new, qn, gn, longn, state_new, dtab, resid)

    slots = branches * taps_count + 1
    back, partial = pl.pallas_call(
        functools.partial(finish_kernel, rows, modes, taps_count, group),
        grid=(blocks,),
        in_specs=[smem, major(rows + 8)] + [major(rows)] * 6 + [major(modes + 3 * (taps_count - 1)), major(modes)] + tail + [anywhere],
        out_specs=[tokens, pl.BlockSpec((slots, SUB, LANES), lambda b: (0, b, 0))],
        out_shape=[wide, jax.ShapeDtypeStruct((slots, blocks * SUB, LANES), F32)],
        scratch_shapes=[scratch(rows)] * 3,
        cost_estimate=cost(150, 8),
        name="finish",
    )(meta_old, xs, ks, vs, gs, dq, dl, dg, turn_in, sums, tapped, dtab, resid, mixed)

    tiles = slots * blocks
    chunk = -(-tiles // ctx_size)
    partial = partial.reshape(tiles, SUB, LANES)
    if chunk * ctx_size > tiles:
        partial = jnp.pad(partial, ((0, chunk * ctx_size - tiles), (0, 0), (0, 0)))
    hops = ctx_size - 1
    summed = pl.pallas_call(
        functools.partial(sum_kernel, ctx_size, chunk),
        in_specs=[whole],
        out_specs=whole,
        out_shape=jax.ShapeDtypeStruct(partial.shape, F32),
        scratch_shapes=[pltpu.VMEM((hops, chunk, SUB, LANES), F32)] + [pltpu.SemaphoreType.DMA((hops,))] * 4,
        compiler_params=pltpu.CompilerParams(collective_id=0, has_side_effects=True),
        name="window_sum",
    )(partial)
    cut = branches * taps_count * blocks
    tap_term = summed[:cut].reshape(branches, taps_count, width)
    filter_term = summed[cut:tiles].reshape(blocks, SUB, modes, LANES // group)
    filter_term = filter_term.transpose(2, 0, 1, 3).reshape(modes, filters)
    return (mixed[None], back[None], filter_term[None], tap_term[None])


def solution(mesh):
    in_specs = (
        P("pipe", "ctx", None),
        P("pipe", "ctx", None),
        P("pipe", "ctx", None),
        P("pipe", None, None, None),
        P("pipe", None, None),
        P("pipe", None, None),
        P(),
    )
    out_specs = (
        P("pipe", "ctx", None),
        P("pipe", "ctx", None),
        P("pipe", None, None),
        P("pipe", None, None, None),
    )

    return jax.shard_map(
        on_device, mesh=mesh, in_specs=in_specs, out_specs=out_specs, check_vma=False
    )
```
